128 devices in a mesh: gx: 8 (over y, x_hi), gy: 8 (over x_lo, z), mem: 2 (over core).
Axes of the slice: x: 4 (x_hi: 2, x_lo: 2; x = x_hi * 2 + x_lo), y: 4, z: 4, core: 2. Of those that a mesh axis runs over, the one named last changes fastest.
Arguments:
- src_hist: bfloat16 [4, 256, 1024, 128], P('mem', 'gx', 'gy'), may hold values from -6 to 6
- rec_p: float32 [256, 1024, 128], P('gx', 'gy'), may hold values from -6 to 6
- rec_q: float32 [256, 1024, 128], P('gx', 'gy'), may hold values from -6 to 6
- prev_p: float32 [256, 1024, 128], P('gx', 'gy'), may hold values from -6 to 6
- prev_q: float32 [256, 1024, 128], P('gx', 'gy'), may hold values from -6 to 6
- horiz: float32 [256, 1024, 128], P('gx', 'gy'), may hold values from 0.04 to 0.12
- vert: float32 [256, 1024, 128], P('gx', 'gy'), may hold values from 0.04 to 0.12
- ratio: float32 [256, 1024, 128], P('gx', 'gy'), may hold values from 0.6 to 1
- tilt: float32 [256, 1024, 128], P('gx', 'gy'), may hold values from -0.4 to 0.4
- rec_pos: int32 [4096], replicated, may hold values from 0 to 33554431
- rec_data: float32 [4, 4096], replicated, may hold values from -6 to 6
- lag_offs: int32 [2, 2], P('mem'), may hold values from -8 to 8, as said below
Outputs:
- image: float32 [2, 256, 1024, 128], P('mem', 'gx', 'gy')
- out_p: float32 [256, 1024, 128], P('gx', 'gy')
- out_q: float32 [256, 1024, 128], P('gx', 'gy')
The draws below stay inside these ranges and needn't reach their ends.
Inputs may be any that keep to these rules, and one draw needn't show every extreme that they name: `lag_offs`: each offset lies within -8 .. 8; the offset pair (8, -8) occurs in every draw.
All inputs are finite; a program needn't handle non-finite values.
Results may differ from the reference program's by a relative error of at most 0.0003.
Values may be sent and summed in bfloat16 or wider, within the bound.
A program may use at most 128 MiB of HBM per device.

```python
import jax
import jax.numpy as jnp
from jax import lax

NZ = 128
NT = 4
HMAX = 8
NLAG = 2
NX = 256
NY = 1024
NREC = 4096


def draw_lag_offs(key, part):
    values = jax.random.randint(key, (NLAG, 2), -HMAX, HMAX + 1, dtype=jnp.int32)
    values = values.at[0, 0].set(HMAX)
    values = values.at[0, 1].set(-HMAX)
    return values.astype(jnp.int32)


def set_ends(result, key, low, top_value):
    dims = result.shape
    place = [jax.random.randint(jax.random.fold_in(key, axis), (), 0, dims[axis]) for axis in range(len(dims))]
    result = result.at[tuple(place)].set(low)
    longest = dims.index(max(dims))
    place[longest] = (place[longest] + 1) % dims[longest]
    return result.at[tuple(place)].set(top_value)


def shard_levels(stream_key, shape, cuts, least, top_value):
    loudness = 1.0
    for axis_at, shards_of in cuts:
        heights = jax.random.uniform(jax.random.fold_in(jax.random.fold_in(stream_key, 6), axis_at), (shards_of,), jnp.float32, least / len(cuts), top_value / len(cuts))
        loudness = loudness * jnp.repeat(jnp.exp(heights), shape[axis_at] // shards_of).reshape((-1,) + (1,) * (len(shape) - 1 - axis_at))
    return loudness


def bell_draw(own_key, shape, width, limit, pieces=(), kind=jnp.bfloat16):
    factor_of = shard_levels(own_key, shape, pieces, -0.22, 0.18) if pieces else 1.0
    values = jax.random.normal(own_key, shape, jnp.float32) * width * factor_of
    return jnp.minimum(jnp.maximum(values, -limit), limit).astype(kind)


def setup_inputs(seed: int = 0) -> dict:
    arg_keys = jax.random.split(jax.random.key(seed), 13)
    return {
        "src_hist": bell_draw(arg_keys[0], (NT, NX, NY, NZ), 1.0, 6.0, ((0, 2), (1, 8), (2, 8))),
        "rec_p": bell_draw(arg_keys[1], (NX, NY, NZ), 1.0, 6.0, ((0, 8), (1, 8)), jnp.float32),
        "rec_q": bell_draw(arg_keys[2], (NX, NY, NZ), 1.0, 6.0, ((0, 8), (1, 8)), jnp.float32),
        "prev_p": bell_draw(arg_keys[3], (NX, NY, NZ), 1.0, 6.0, ((0, 8), (1, 8)), jnp.float32),
        "prev_q": bell_draw(arg_keys[4], (NX, NY, NZ), 1.0, 6.0, ((0, 8), (1, 8)), jnp.float32),
        "horiz": jnp.clip(0.04 + 0.08 * jax.random.uniform(arg_keys[5], (NX, NY, NZ), jnp.float32) ** shard_levels(arg_keys[5], (NX, NY, NZ), ((0, 8), (1, 8)), -0.2, 0.2), 0.04, 0.12),
        "vert": jnp.clip(0.04 + 0.08 * jax.random.uniform(arg_keys[6], (NX, NY, NZ), jnp.float32) ** shard_levels(arg_keys[6], (NX, NY, NZ), ((0, 8), (1, 8)), -0.2, 0.2), 0.04, 0.12),
        "ratio": jnp.clip(0.6 + 0.39999998 * jax.random.uniform(arg_keys[7], (NX, NY, NZ), jnp.float32) ** shard_levels(arg_keys[7], (NX, NY, NZ), ((0, 8), (1, 8)), -0.2, 0.2), 0.6, 1.0),
        "tilt": jnp.clip(jax.random.uniform(arg_keys[8], (NX, NY, NZ), jnp.float32, -0.4, 0.4) * shard_levels(arg_keys[8], (NX, NY, NZ), ((0, 8), (1, 8)), -0.4, 0.0), -0.4, 0.4),
        "rec_pos": set_ends(jax.random.randint(arg_keys[9], (NREC,), 0, NX * NY * NZ), jax.random.fold_in(arg_keys[9], 1), 0, (NX * NY * NZ) - 1).astype(jnp.int32),
        "rec_data": bell_draw(arg_keys[10], (NT, NREC), 1.0, 6.0, (), jnp.float32),
        "lag_offs": draw_lag_offs(jax.random.fold_in(arg_keys[12], 71), 0),
    }


def advance(p, q, old_p, old_q, wide_p, wide_q, horiz, vert, ratio, tilt):
    lateral = wide_p[2:, 1:-1] + wide_p[:-2, 1:-1] + wide_p[1:-1, 2:] + wide_p[1:-1, :-2] - 4.0 * p
    deep = jnp.pad(wide_q[:, 1:-1], ((0, 0), (0, 0), (1, 1)))
    center = deep[1:-1]
    second = center[:, :, 2:] + center[:, :, :-2] - 2.0 * q
    mixed = 0.25 * (deep[2:, :, 2:] - deep[2:, :, :-2] - deep[:-2, :, 2:] + deep[:-2, :, :-2])
    horizontal = horiz * lateral
    upright = vert * (second + tilt * mixed)
    new_p = 2.0 * p - old_p + horizontal + upright
    new_q = 2.0 * q - old_q + ratio * horizontal + upright
    return new_p, new_q


def reference(src_hist, rec_p, rec_q, prev_p, prev_q, horiz, vert, ratio, tilt, rec_pos, rec_data, lag_offs):
    shape = rec_p.shape
    fields = jnp.stack([rec_p, rec_q])
    older = jnp.stack([prev_p, prev_q])
    image = jnp.zeros((lag_offs.shape[0],) + shape, jnp.float32)

    def advance_step(carry, k):
        fields, older, image = carry
        t = NT - 1 - k
        snap = lax.dynamic_index_in_dim(src_hist, t, 0, keepdims=False)
        wide_s = jnp.pad(snap, ((HMAX, HMAX), (HMAX, HMAX), (0, 0)))
        current = fields[0]

        def one_lag(offset):
            piece = lax.dynamic_slice(wide_s, (HMAX - offset[0], HMAX - offset[1], jnp.int32(0)), shape)
            return piece.astype(jnp.float32) * current

        image = image + lax.map(one_lag, lag_offs)
        wide = jnp.pad(fields, ((0, 0), (1, 1), (1, 1), (0, 0)))
        new_p, new_q = advance(fields[0], fields[1], older[0], older[1], wide[0], wide[1], horiz, vert, ratio, tilt)
        amount = lax.dynamic_index_in_dim(rec_data, t, 0, keepdims=False)
        new_p = new_p.reshape(-1).at[rec_pos].add(amount).reshape(shape)
        new_q = new_q.reshape(-1).at[rec_pos].add(amount).reshape(shape)
        return (jnp.stack([new_p, new_q]), fields, image), None

    (fields, older, image), unused = lax.scan(advance_step, (fields, older, image), jnp.arange(NT, dtype=jnp.int32))
    return image, fields[0], fields[1]
```

```python
import functools

import jax
import jax.numpy as jnp
from jax import lax
from jax.experimental import pallas as pl
from jax.experimental.pallas import tpu as pltpu
from jax.sharding import PartitionSpec as P

NT = 4
HMAX = 8
PAD = 8
CHUNK = 32
MESH = pl.DeviceIdType.MESH


def log2(n):
    bits = n.bit_length() - 1
    assert 1 << bits == n
    return bits


def inject_kernel(counts, pos_v, pos_s, data_s, out, link_v, link_s, sem):
    _, width_x, width_y, depth = out.shape
    rows = pos_v.shape[0]
    total = rows * 128
    bits_z, bits_y, bits_x = log2(depth), log2(width_y), log2(width_x)
    bits_gy = log2(counts[1])
    pos = pos_v[...]
    block_y = (pos >> (bits_z + bits_y)) & (counts[1] - 1)
    block_x = pos >> (bits_z + bits_y + bits_gy + bits_x)
    inside = (block_x == lax.axis_index("gx")) & (block_y == lax.axis_index("gy"))
    lane = lax.broadcasted_iota(jnp.int32, (rows, 128), 1)
    row = lax.broadcasted_iota(jnp.int32, (rows, 128), 0)
    link = jnp.where(inside, row * 128 + lane, total)
    step = 1
    while step < 128:
        ahead = pltpu.roll(link, 128 - step, 1)
        link = jnp.minimum(link, jnp.where(lane < 128 - step, ahead, total))
        step *= 2
    later = jnp.broadcast_to(link[:, :1], (rows, 128))
    later = jnp.where(row < rows - 1, pltpu.roll(later, rows - 1, 0), total)
    step = 1
    while step < rows:
        ahead = pltpu.roll(later, rows - step, 0)
        later = jnp.minimum(later, jnp.where(row < rows - step, ahead, total))
        step *= 2
    link_v[...] = jnp.minimum(link, later)
    copy = pltpu.make_async_copy(link_v, link_s, sem)
    copy.start()

    def clear(x, carry):
        for t in range(NT):
            out[t, x] = jnp.zeros((width_y, depth), jnp.float32)
        return carry

    lax.fori_loop(0, width_x, clear, 0)
    copy.wait()
    cell = lax.broadcasted_iota(jnp.int32, (1, depth), 1)

    def add(r):
        where = pos_s[r]
        x = (where >> (bits_z + bits_y + bits_gy)) & (width_x - 1)
        y = (where >> bits_z) & (width_y - 1)
        z = where & (depth - 1)
        hit = cell == z
        for t in range(NT):
            line = out[t, x, pl.ds(y, 1), :]
            out[t, x, pl.ds(y, 1), :] = line + jnp.where(hit, data_s[NT - 1 - t, r], 0.0)
        after = jnp.minimum(r + 1, total - 1)
        return jnp.where(r + 1 < total, link_s[after >> 7, after & 127], total)

    lax.while_loop(lambda r: r < total, add, link_s[0, 0])


def inject(counts, rec_pos, rec_data, shape):
    total = rec_pos.shape[0]
    rows = total // 128
    return pl.pallas_call(
        functools.partial(inject_kernel, counts),
        out_shape=jax.ShapeDtypeStruct((NT,) + shape, jnp.float32),
        in_specs=[
            pl.BlockSpec(memory_space=pltpu.VMEM),
            pl.BlockSpec(memory_space=pltpu.SMEM),
            pl.BlockSpec(memory_space=pltpu.SMEM),
        ],
        out_specs=pl.BlockSpec(memory_space=pltpu.VMEM),
        scratch_shapes=[
            pltpu.VMEM((rows, 128), jnp.int32),
            pltpu.SMEM((rows, 128), jnp.int32),
            pltpu.SemaphoreType.DMA,
        ],
        compiler_params=pltpu.CompilerParams(vmem_limit_bytes=20 << 20),
        name="inject",
    )(rec_pos.reshape(rows, 128), rec_pos, rec_data)


def march_kernel(
    counts,
    lag,
    src,
    rec_p,
    rec_q,
    prev_p,
    prev_q,
    horiz,
    vert,
    ratio,
    tilt,
    inj,
    image_out,
    p_out,
    q_out,
    f0, f1, f2, f3, f4,
    qa, qb,
    ch, cv, cr, ct,
    cinj,
    img,
    sx0, sx1, sx2, sx3,
    yl0, yl1, yl2, yl3,
    yr0, yr1, yr2, yr3,
    wide,
    xsend, xrecv, ysend, yrecv,
    load_sem,
    sx_sem, sy_sem, sc_sem, sm_sem,
    px_sem, py_sem,
    out_sem,
):
    n_gx, n_gy = counts
    gx, gy, mem = lax.axis_index("gx"), lax.axis_index("gy"), lax.axis_index("mem")
    width_x, width_y, depth = rec_p.shape
    last = width_x - 1
    sx = (sx0, sx1, sx2, sx3)
    yl = (yl0, yl1, yl2, yl3)
    yr = (yr0, yr1, yr2, yr3)
    own = pl.ds(HMAX, width_x)
    rows_in = pl.ds(PAD, width_y)

    loads = []

    def load(source, dest):
        copy = pltpu.make_async_copy(source, dest, load_sem.at[len(loads)])
        copy.start()
        loads.append(copy)

    load(rec_p, f0.at[:, rows_in])
    load(rec_q, qa)
    load(prev_p, f1.at[:, rows_in])
    load(horiz, ch)
    load(vert, cv)
    load(tilt, ct)
    load(prev_q, qb)
    load(ratio, cr)
    load(inj, cinj)
    load(src.at[0], sx0.at[own])
    load(src.at[1], sx1.at[own])

    def at(dgx, dgy):
        return ((gx + dgx + n_gx) % n_gx, (gy + dgy + n_gy) % n_gy, mem)

    peer = (gx, gy, 1 - mem)
    barrier = pltpu.get_barrier_semaphore()
    around = [(a, b) for a in (-1, 0, 1) for b in (-1, 0, 1) if (a, b) != (0, 0)]
    for a, b in around:
        pl.semaphore_signal(barrier, inc=1, device_id=at(a, b), device_id_type=MESH)
    pl.semaphore_signal(barrier, inc=1, device_id=peer, device_id_type=MESH)

    def exists(a, b):
        ok = True
        if a == -1:
            ok = gx > 0
        if a == 1:
            ok = gx < n_gx - 1
        if b == -1:
            ok_y = gy > 0
        if b == 1:
            ok_y = gy < n_gy - 1
        if b == 0:
            return ok
        if a == 0:
            return ok_y
        return ok & ok_y

    zero_row = jnp.zeros((1, depth), jnp.float32)

    def clear_pads(x, carry):
        for f in (f0, f1, f2, f3):
            f[x, PAD - 1 : PAD, :] = zero_row
            f[x, PAD + width_y : PAD + width_y + 1, :] = zero_row
        return carry

    lax.fori_loop(0, width_x, clear_pads, 0)

    spans = {-1: (0, HMAX), 0: (HMAX, width_x), 1: (HMAX + width_x, HMAX)}
    for j in range(2):
        for a in (-1, 1):
            first, n = spans[a]

            @pl.when(jnp.logical_not(exists(a, 0)))
            def _(j=j, first=first, n=n):
                for x in range(n):
                    sx[j][first + x] = jnp.zeros((width_y, depth), jnp.bfloat16)

        for b, side in ((-1, yl), (1, yr)):
            for a in (-1, 0, 1):
                first, n = spans[a]

                @pl.when(jnp.logical_not(exists(a, b)))
                def _(j=j, first=first, n=n, side=side):
                    def clear(x, carry):
                        side[j][first + x] = jnp.zeros((HMAX, depth), jnp.bfloat16)
                        return carry

                    lax.fori_loop(0, n, clear, 0)

    for a, side in ((-1, 0), (1, 1)):

        @pl.when(jnp.logical_not(exists(a, 0)))
        def _(side=side):
            for k in range(NT):
                for f in range(2):
                    xrecv[k, side, f] = jnp.zeros((width_y, depth), jnp.bfloat16)

        @pl.when(jnp.logical_not(exists(0, a)))
        def _(side=side):
            for k in range(NT):
                yrecv[k, side] = jnp.zeros((width_x, depth), jnp.float32)

    pl.semaphore_wait(barrier, len(around) + 1)

    def remote(source, dest, sems, i, target):
        return pltpu.make_async_remote_copy(
            src_ref=source,
            dst_ref=dest,
            send_sem=sems.at[0, i],
            recv_sem=sems.at[1, i],
            device_id=target,
            device_id_type=MESH,
        )

    def begin(a, b, copy):
        @pl.when(exists(a, b))
        def _():
            copy().start()

    def sent(a, b, copy):
        @pl.when(exists(a, b))
        def _():
            copy().wait_send()

    def landed(a, b, copy):
        @pl.when(exists(-a, -b))
        def _():
            copy().wait_recv()

    def edge(a, size):
        return pl.ds(size - HMAX, HMAX) if a == 1 else pl.ds(0, HMAX)

    def halo_x(a):
        first, n = spans[-a]
        return pl.ds(first, n)

    def source_x(j, a):
        i = j * 2 + (a + 1) // 2
        return lambda: remote(
            src.at[j, edge(a, width_x)], sx[j].at[halo_x(a)], sx_sem, i, at(a, 0)
        )

    def source_y(j, b):
        i = j * 2 + (b + 1) // 2
        dest = yl if b == 1 else yr
        return lambda: remote(
            src.at[j, :, edge(b, width_y)], dest[j].at[own], sy_sem, i, at(0, b)
        )

    def source_corner(j, a, b):
        i = j * 4 + (a + 1) + (b + 1) // 2
        dest = yl if b == 1 else yr
        return lambda: remote(
            src.at[j, edge(a, width_x), edge(b, width_y)],
            dest[j].at[halo_x(a)],
            sc_sem,
            i,
            at(a, b),
        )

    def to_peer(j, part):
        if part == 0:
            return remote(src.at[j], sx[2 + j].at[own], sm_sem, j, peer)
        if part == 1:
            here, there = sx[j].at[pl.ds(*spans[-1])], sx[2 + j].at[pl.ds(*spans[-1])]
        if part == 2:
            here, there = sx[j].at[pl.ds(*spans[1])], sx[2 + j].at[pl.ds(*spans[1])]
        if part == 3:
            here, there = yl[j], yl[2 + j]
        if part == 4:
            here, there = yr[j], yr[2 + j]
        return remote(here, there, sm_sem, part * 2 + j, peer)

    def field_x(k, a):
        side = (a + 1) // 2
        return lambda: remote(
            xsend.at[k, side], xrecv.at[k, 1 - side], px_sem, k * 2 + side, at(a, 0)
        )

    def field_y(k, b):
        side = (b + 1) // 2
        return lambda: remote(
            ysend.at[k, side], yrecv.at[k, 1 - side], py_sem, k * 2 + side, at(0, b)
        )

    fields = (f0, f1, f2, f3, f4)
    qs = (qa, qb)

    def stage_edges(k, p, q, rows):
        for side, x in ((0, 0), (1, last)):
            for y in range(0, width_y, CHUNK):
                xsend[k, side, 0, y : y + CHUNK, :] = p[
                    x, PAD + y : PAD + y + CHUNK, :
                ].astype(jnp.bfloat16)
                xsend[k, side, 1, y : y + CHUNK, :] = q[x, y : y + CHUNK, :].astype(
                    jnp.bfloat16
                )
        for a in (1, -1):
            begin(a, 0, field_x(k, a))
        if rows:

            def stage(x, carry):
                ysend[k, 0, pl.ds(x, 1), :] = p[x, PAD : PAD + 1, :]
                ysend[k, 1, pl.ds(x, 1), :] = p[x, PAD + width_y - 1 : PAD + width_y, :]
                return carry

            lax.fori_loop(0, width_x, stage, 0)
        for b in (1, -1):
            begin(0, b, field_y(k, b))

    lane = lax.broadcasted_iota(jnp.int32, (CHUNK, depth), 1)
    has_above = lane < depth - 1
    has_below = lane > 0

    def above(v):
        return jnp.where(has_above, pltpu.roll(v, depth - 1, 1), 0.0)

    def below(v):
        return jnp.where(has_below, pltpu.roll(v, 1, 1), 0.0)

    def plane(k, x, before, after):
        p, q = fields[k], qs[k % 2]
        old_p = fields[1] if k == 0 else fields[k - 1]
        new_p, new_q = fields[k + 1], qs[(k + 1) % 2]
        for y in range(0, width_y, CHUNK):
            own_rows = slice(y, y + CHUNK)
            pad_rows = slice(PAD + y, PAD + y + CHUNK)
            pc = p[x, pad_rows, :]
            lateral = (
                after(0, y)
                + before(0, y)
                + p[x, PAD + y + 1 : PAD + y + 1 + CHUNK, :]
                + p[x, PAD + y - 1 : PAD + y - 1 + CHUNK, :]
                - 4.0 * pc
            )
            qc = q[x, own_rows, :]
            slope = 0.25 * (after(1, y) - before(1, y))
            second = above(qc) + below(qc) - 2.0 * qc
            mixed = above(slope) - below(slope)
            added = cinj[k, x, own_rows, :]
            upright = cv[x, own_rows, :] * (second + ct[x, own_rows, :] * mixed) + added
            horizontal = ch[x, own_rows, :] * lateral
            new_p[x, pad_rows, :] = (2.0 * pc - old_p[x, pad_rows, :]) + horizontal + upright
            new_q[x, own_rows, :] = (
                (2.0 * qc - new_q[x, own_rows, :])
                + cr[x, own_rows, :] * horizontal
                + upright
            )

    def near(k, x):
        p, q = fields[k], qs[k % 2]

        def get(which, y):
            if which == 0:
                return p[x, PAD + y : PAD + y + CHUNK, :]
            return q[x, y : y + CHUNK, :]

        return get

    def far(k, side):
        def get(which, y):
            return xrecv[k, side, which, y : y + CHUNK, :].astype(jnp.float32)

        return get

    def mend(k):
        new_p, new_q = fields[k + 1], qs[(k + 1) % 2]

        def one(x, carry):
            for side, y in ((0, 0), (1, width_y - 1)):
                part = ch[x, y : y + 1, :] * yrecv[k, side, pl.ds(x, 1), :]
                line = new_p[x, PAD + y : PAD + y + 1, :] + part
                new_p[x, PAD + y : PAD + y + 1, :] = line
                if k < NT - 1:
                    ysend[k + 1, side, pl.ds(x, 1), :] = line
                new_q[x, y : y + 1, :] += cr[x, y : y + 1, :] * part
            return carry

        lax.fori_loop(0, width_x, one, 0, unroll=4)

    loads[0].wait()
    loads[1].wait()
    stage_edges(0, f0, qa, True)
    for j in range(2):
        to_peer(j, 0).start()
    for j in range(2):
        for a in (1, -1):
            for b in (1, -1):
                begin(a, b, source_corner(j, a, b))
        for b in (1, -1):
            begin(0, b, source_y(j, b))
    for copy in loads[2:]:
        copy.wait()

    for k in range(NT):
        j, a = k // 2, (1, -1)[k % 2]
        begin(a, 0, source_x(j, a))

        def inner(x, carry, k=k):
            plane(k, x, near(k, x - 1), near(k, x + 1))
            return carry

        lax.fori_loop(1, last, inner, 0)
        for side in (1, -1):
            landed(side, 0, field_x(k, side))
        plane(k, 0, far(k, 0), near(k, 1))
        plane(k, last, near(k, last - 1), far(k, 1))
        for side in (1, -1):
            landed(0, side, field_y(k, side))
        mend(k)
        if k < NT - 1:
            stage_edges(k + 1, fields[k + 1], qs[(k + 1) % 2], False)
        if k == 1:
            for j in range(2):
                for b in (1, -1):
                    landed(0, b, source_y(j, b))
                    for a in (1, -1):
                        landed(a, b, source_corner(j, a, b))
                for part in (3, 4):
                    to_peer(j, part).start()
        if k == 2:
            for a in (1, -1):
                landed(a, 0, source_x(0, a))
            for part in (1, 2):
                to_peer(0, part).start()

    outs = [
        pltpu.make_async_copy(f4.at[:, rows_in], p_out, out_sem.at[0]),
        pltpu.make_async_copy(qs[NT % 2], q_out, out_sem.at[1]),
    ]
    for copy in outs:
        copy.start()

    for a in (1, -1):
        landed(a, 0, source_x(1, a))
    for part in (1, 2):
        to_peer(1, part).start()
    for part in range(5):
        for j in range(2):
            to_peer(j, part).wait_recv()

    shift_x = lag[0, 0]
    shift_y = lag[0, 1]

    def times(s):
        return (2 * mem + s) if s < 2 else (2 * (1 - mem) + s - 2)

    def imaging(low):
        def by_plane(x, carry):
            at_x = x + HMAX - shift_x
            for s in range(4):
                wide[s, 0:HMAX, :] = yl[s][at_x].astype(jnp.float32)
                wide[s, HMAX : HMAX + width_y, :] = sx[s][at_x].astype(jnp.float32)
                wide[s, HMAX + width_y : 2 * HMAX + width_y, :] = yr[s][at_x].astype(
                    jnp.float32
                )
            for y in range(0, width_y, CHUNK):
                total = None
                for s in range(4):
                    k = NT - 1 - ((2 * low + s) if s < 2 else (2 * (1 - low) + s - 2))
                    piece = wide[s, pl.ds(HMAX - shift_y + y, CHUNK), :]
                    term = piece * fields[k][x, PAD + y : PAD + y + CHUNK, :]
                    total = term if total is None else total + term
                img[x, y : y + CHUNK, :] = total
            return carry

        lax.fori_loop(0, width_x, by_plane, 0)

    for m in range(2):

        @pl.when(mem == m)
        def _(m=m):
            imaging(m)

    outs.append(pltpu.make_async_copy(img, image_out.at[0], out_sem.at[2]))
    outs[-1].start()

    for k in range(NT):
        for a in (1, -1):
            sent(a, 0, field_x(k, a))
            sent(0, a, field_y(k, a))
    for j in range(2):
        for a in (1, -1):
            sent(a, 0, source_x(j, a))
            sent(0, a, source_y(j, a))
            for b in (1, -1):
                sent(a, b, source_corner(j, a, b))
        for part in range(5):
            to_peer(j, part).wait_send()
    for copy in outs:
        copy.wait()


def march(counts, lag, src, rec_p, rec_q, prev_p, prev_q, horiz, vert, ratio, tilt, inj):
    shape = rec_p.shape
    width_x, width_y, depth = shape
    padded = (width_x, width_y + 2 * PAD, depth)
    f32, bf16 = jnp.float32, jnp.bfloat16
    hbm = pl.BlockSpec(memory_space=pl.ANY)
    scratch = (
        [pltpu.VMEM(padded, f32)] * 5
        + [pltpu.VMEM(shape, f32)] * 2
        + [pltpu.VMEM(shape, f32)] * 4
        + [pltpu.VMEM((NT,) + shape, f32)]
        + [pltpu.VMEM(shape, f32)]
        + [pltpu.VMEM((width_x + 2 * HMAX, width_y, depth), bf16)] * 4
        + [pltpu.VMEM((width_x + 2 * HMAX, HMAX, depth), bf16)] * 8
        + [pltpu.VMEM((4, width_y + 2 * HMAX, depth), f32)]
        + [pltpu.VMEM((NT, 2, 2, width_y, depth), bf16)] * 2
        + [pltpu.VMEM((NT, 2, width_x, depth), f32)] * 2
        + [pltpu.SemaphoreType.DMA((11,))]
        + [pltpu.SemaphoreType.DMA((2, n)) for n in (4, 4, 8, 10, 2 * NT, 2 * NT)]
        + [pltpu.SemaphoreType.DMA((3,))]
    )
    return pl.pallas_call(
        functools.partial(march_kernel, counts),
        out_shape=(
            jax.ShapeDtypeStruct((1,) + shape, f32),
            jax.ShapeDtypeStruct(shape, f32),
            jax.ShapeDtypeStruct(shape, f32),
        ),
        in_specs=[pl.BlockSpec(memory_space=pltpu.SMEM)] + [hbm] * 10,
        out_specs=(hbm, hbm, hbm),
        scratch_shapes=scratch,
        compiler_params=pltpu.CompilerParams(
            collective_id=0, has_side_effects=True, vmem_limit_bytes=58 << 20
        ),
        name="march",
    )(lag, src, rec_p, rec_q, prev_p, prev_q, horiz, vert, ratio, tilt, inj)


def solution(mesh):
    counts = (mesh.shape["gx"], mesh.shape["gy"])

    def body(
        src_hist, rec_p, rec_q, prev_p, prev_q, horiz, vert, ratio, tilt, rec_pos, rec_data, lag_offs
    ):
        added = inject(counts, rec_pos, rec_data, rec_p.shape)
        return march(
            counts, lag_offs, src_hist, rec_p, rec_q, prev_p, prev_q, horiz, vert, ratio, tilt, added
        )

    cells = P("gx", "gy", None)
    return jax.shard_map(
        body,
        mesh=mesh,
        in_specs=(P("mem", "gx", "gy", None),) + (cells,) * 8 + (P(), P(), P("mem", None)),
        out_specs=(P("mem", "gx", "gy", None), cells, cells),
        check_vma=False,
    )
```

```python
import functools

import jax
import jax.numpy as jnp
from jax import lax
from jax.experimental import pallas as pl
from jax.experimental.pallas import tpu as pltpu
from jax.sharding import PartitionSpec as P

NT = 4
HMAX = 8
PAD = 8
PIECE = 4
REACHES = (0, 4, 8)
CHUNK = 32
MESH = pl.DeviceIdType.MESH


def log2(n):
    bits = n.bit_length() - 1
    assert 1 << bits == n
    return bits


def inject_kernel(
    counts, pos_rows, pos, data, out, pos_v, pos_s, data_s, link_v, link_s, sem
):
    _, width_x, width_y, depth = out.shape
    staged = [
        pltpu.make_async_copy(here, there, sem.at[i])
        for i, (here, there) in enumerate(((pos_rows, pos_v), (pos, pos_s), (data, data_s)))
    ]
    for copy in staged:
        copy.start()

    def clear(x, carry):
        for t in range(NT):
            out[t, x] = jnp.zeros((width_y, depth), jnp.float32)
        return carry

    lax.fori_loop(0, width_x // 2, clear, 0)
    rows = pos_v.shape[0]
    total = rows * 128
    bits_z, bits_y, bits_x = log2(depth), log2(width_y), log2(width_x)
    bits_gy = log2(counts[1])
    staged[0].wait()
    place = pos_v[...]
    block_y = (place >> (bits_z + bits_y)) & (counts[1] - 1)
    block_x = place >> (bits_z + bits_y + bits_gy + bits_x)
    inside = (block_x == lax.axis_index("gx")) & (block_y == lax.axis_index("gy"))
    lane = lax.broadcasted_iota(jnp.int32, (rows, 128), 1)
    row = lax.broadcasted_iota(jnp.int32, (rows, 128), 0)
    link = jnp.where(inside, row * 128 + lane, total)
    step = 1
    while step < 128:
        ahead = pltpu.roll(link, 128 - step, 1)
        link = jnp.minimum(link, jnp.where(lane < 128 - step, ahead, total))
        step *= 2
    later = jnp.broadcast_to(link[:, :1], (rows, 128))
    later = jnp.where(row < rows - 1, pltpu.roll(later, rows - 1, 0), total)
    step = 1
    while step < rows:
        ahead = pltpu.roll(later, rows - step, 0)
        later = jnp.minimum(later, jnp.where(row < rows - step, ahead, total))
        step *= 2
    link_v[...] = jnp.minimum(link, later)
    copy = pltpu.make_async_copy(link_v, link_s, sem.at[3])
    copy.start()
    lax.fori_loop(width_x // 2, width_x, clear, 0)
    copy.wait()
    for copy in staged[1:]:
        copy.wait()
    cell = lax.broadcasted_iota(jnp.int32, (1, depth), 1)

    def add(r):
        where = pos_s[r]
        x = (where >> (bits_z + bits_y + bits_gy)) & (width_x - 1)
        y = (where >> bits_z) & (width_y - 1)
        z = where & (depth - 1)
        hit = cell == z
        for t in range(NT):
            line = out[t, x, pl.ds(y, 1), :]
            out[t, x, pl.ds(y, 1), :] = line + jnp.where(hit, data_s[NT - 1 - t, r], 0.0)
        after = jnp.minimum(r + 1, total - 1)
        return jnp.where(r + 1 < total, link_s[after >> 7, after & 127], total)

    lax.while_loop(lambda r: r < total, add, link_s[0, 0])


def inject(counts, rec_pos, rec_data, shape):
    total = rec_pos.shape[0]
    rows = total // 128
    return pl.pallas_call(
        functools.partial(inject_kernel, counts),
        out_shape=jax.ShapeDtypeStruct((NT,) + shape, jnp.float32),
        in_specs=[pl.BlockSpec(memory_space=pltpu.HBM)] * 3,
        out_specs=pl.BlockSpec(memory_space=pltpu.VMEM),
        scratch_shapes=[
            pltpu.VMEM((rows, 128), jnp.int32),
            pltpu.SMEM((total,), jnp.int32),
            pltpu.SMEM(rec_data.shape, jnp.float32),
            pltpu.VMEM((rows, 128), jnp.int32),
            pltpu.SMEM((rows, 128), jnp.int32),
            pltpu.SemaphoreType.DMA((4,)),
        ],
        compiler_params=pltpu.CompilerParams(vmem_limit_bytes=20 << 20),
        name="inject",
    )(
        *(
            pltpu.with_memory_space_constraint(v, pltpu.HBM)
            for v in (rec_pos.reshape(rows, 128), rec_pos, rec_data)
        )
    )


def march_kernel(
    counts,
    reach,
    lag,
    src,
    rec_p,
    rec_q,
    prev_p,
    prev_q,
    horiz,
    vert,
    ratio,
    tilt,
    inj,
    image_out,
    p_out,
    q_out,
    f0, f1, f2, f3,
    qa, qb,
    ch, cv, cr, ct,
    sx0, sx1, sx2, sx3,
    yl0, yl1, yl2, yl3,
    yr0, yr1, yr2, yr3,
    wide,
    xsend, xrecv, ysend, yrecv,
    load_sem,
    sx_sem, sy_sem, sc_sem, sm_sem,
    px_sem, py_sem,
):
    n_gx, n_gy = counts
    gx, gy, mem = lax.axis_index("gx"), lax.axis_index("gy"), lax.axis_index("mem")
    width_x, width_y, depth = rec_p.shape
    last = width_x - 1
    sx = (sx0, sx1, sx2, sx3)
    yl = (yl0, yl1, yl2, yl3)
    yr = (yr0, yr1, yr2, yr3)
    own = pl.ds(HMAX, width_x)
    rows_in = pl.ds(PAD, width_y)

    loads = []

    def load(source, dest):
        copy = pltpu.make_async_copy(source, dest, load_sem.at[len(loads)])
        copy.start()
        loads.append(copy)

    load(rec_p, f0.at[:, rows_in])
    load(rec_q, qa)
    load(prev_p, f1.at[:, rows_in])
    load(horiz, ch)
    load(vert, cv)
    load(tilt, ct)
    load(prev_q, qb)
    load(ratio, cr)
    load(src.at[0], sx0.at[own])
    load(src.at[1], sx1.at[own])

    def at(dgx, dgy):
        return ((gx + dgx + n_gx) % n_gx, (gy + dgy + n_gy) % n_gy, mem)

    peer = (gx, gy, 1 - mem)
    barrier = pltpu.get_barrier_semaphore()
    around = [(a, b) for a in (-1, 0, 1) for b in (-1, 0, 1) if (a, b) != (0, 0)]
    for a, b in around:
        pl.semaphore_signal(barrier, inc=1, device_id=at(a, b), device_id_type=MESH)
    pl.semaphore_signal(barrier, inc=1, device_id=peer, device_id_type=MESH)

    def exists(a, b):
        ok = True
        if a == -1:
            ok = gx > 0
        if a == 1:
            ok = gx < n_gx - 1
        if b == -1:
            ok_y = gy > 0
        if b == 1:
            ok_y = gy < n_gy - 1
        if b == 0:
            return ok
        if a == 0:
            return ok_y
        return ok & ok_y

    zero_row = jnp.zeros((1, depth), jnp.float32)

    def clear_pads(x, carry):
        for f in (f0, f1, f2, f3):
            f[x, PAD - 1 : PAD, :] = zero_row
            f[x, PAD + width_y : PAD + width_y + 1, :] = zero_row
        return carry

    lax.fori_loop(0, width_x, clear_pads, 0)

    spans = {-1: (0, HMAX), 0: (HMAX, width_x), 1: (HMAX + width_x, reach)}
    sides = (1, -1) if reach else (1,)
    for j in range(2):
        for a in (-1, 1):
            first, n = spans[a]

            @pl.when(jnp.logical_not(exists(a, 0)))
            def _(j=j, first=first, n=n):
                for x in range(n):
                    sx[j][first + x] = jnp.zeros((width_y, depth), jnp.bfloat16)

        for b, side in ((-1, yl), (1, yr)):
            for a in (-1, 0, 1):
                first, n = spans[a]
                if not n:
                    continue

                @pl.when(jnp.logical_not(exists(a, b)))
                def _(j=j, first=first, n=n, side=side):
                    def clear(x, carry):
                        side[j][first + x] = jnp.zeros((HMAX, depth), jnp.bfloat16)
                        return carry

                    lax.fori_loop(0, n, clear, 0)

    for a, side in ((-1, 0), (1, 1)):

        @pl.when(jnp.logical_not(exists(a, 0)))
        def _(side=side):
            for k in range(NT):
                for f in range(2):
                    xrecv[k, side, f] = jnp.zeros((width_y, depth), jnp.bfloat16)

        @pl.when(jnp.logical_not(exists(0, a)))
        def _(side=side):
            for k in range(NT):
                yrecv[k, side] = jnp.zeros((width_x, depth), jnp.float32)

    def remote(source, dest, sems, i, target):
        return pltpu.make_async_remote_copy(
            src_ref=source,
            dst_ref=dest,
            send_sem=sems.at[0, i],
            recv_sem=sems.at[1, i],
            device_id=target,
            device_id_type=MESH,
        )

    def begin(a, b, copy):
        @pl.when(exists(a, b))
        def _():
            copy().start()

    def sent(a, b, copy):
        @pl.when(exists(a, b))
        def _():
            copy().wait_send()

    def landed(a, b, copy):
        @pl.when(exists(-a, -b))
        def _():
            copy().wait_recv()

    def edge_x(a):
        return pl.ds(width_x - HMAX, HMAX) if a == 1 else pl.ds(0, reach)

    def edge_y(b):
        return pl.ds(width_y - HMAX, HMAX) if b == 1 else pl.ds(0, HMAX)

    def halo_x(a):
        first, n = spans[-a]
        return pl.ds(first, n)

    def source_x(j, a, part):
        i = j * 4 + (a + 1) + part
        first = width_x - HMAX if a == 1 else 0
        return lambda: remote(
            src.at[j, pl.ds(first + part * PIECE, PIECE)],
            sx[j].at[pl.ds(spans[-a][0] + part * PIECE, PIECE)],
            sx_sem,
            i,
            at(a, 0),
        )

    halves = (1, 2) if reach else (1,)
    parts = (0,) + halves + (3, 4)
    pieces = [
        [(j, a, part) for part in range(2) for a in sides if part * PIECE < spans[-a][1]]
        for j in range(2)
    ]

    def source_y(j, b):
        i = j * 2 + (b + 1) // 2
        dest = yl if b == 1 else yr
        return lambda: remote(
            src.at[j, :, edge_y(b)], dest[j].at[own], sy_sem, i, at(0, b)
        )

    def source_corner(j, a, b):
        i = j * 4 + (a + 1) + (b + 1) // 2
        dest = yl if b == 1 else yr
        return lambda: remote(
            src.at[j, edge_x(a), edge_y(b)],
            dest[j].at[halo_x(a)],
            sc_sem,
            i,
            at(a, b),
        )

    def to_peer(j, part):
        if part == 0:
            return remote(src.at[j], sx[2 + j].at[own], sm_sem, j, peer)
        if part == 1:
            here, there = sx[j].at[pl.ds(*spans[-1])], sx[2 + j].at[pl.ds(*spans[-1])]
        if part == 2:
            here, there = sx[j].at[pl.ds(*spans[1])], sx[2 + j].at[pl.ds(*spans[1])]
        used = pl.ds(0, HMAX + width_x + reach)
        if part == 3:
            here, there = yl[j].at[used], yl[2 + j].at[used]
        if part == 4:
            here, there = yr[j].at[used], yr[2 + j].at[used]
        return remote(here, there, sm_sem, part * 2 + j, peer)

    def field_x(k, a):
        side = (a + 1) // 2
        return lambda: remote(
            xsend.at[k, side], xrecv.at[k, 1 - side], px_sem, k * 2 + side, at(a, 0)
        )

    def field_y(k, b):
        side = (b + 1) // 2
        return lambda: remote(
            ysend.at[k, side], yrecv.at[k, 1 - side], py_sem, k * 2 + side, at(0, b)
        )

    fields = (f0, f1, f2, f3, p_out)
    qs = (qa, qb, qa, qb, q_out)
    pads = (PAD, PAD, PAD, PAD, 0)

    def stage_planes(k):
        p, q = fields[k], qs[k]
        for side, x in ((0, 0), (1, last)):
            for y in range(0, width_y, CHUNK):
                xsend[k, side, 0, y : y + CHUNK, :] = p[
                    x, PAD + y : PAD + y + CHUNK, :
                ].astype(jnp.bfloat16)
                xsend[k, side, 1, y : y + CHUNK, :] = q[x, y : y + CHUNK, :].astype(
                    jnp.bfloat16
                )

    def send_planes(k):
        for a in (1, -1):
            begin(a, 0, field_x(k, a))

    def stage_rows(k):
        p = fields[k]

        def stage(x, carry):
            ysend[k, 0, pl.ds(x, 1), :] = p[x, PAD : PAD + 1, :]
            ysend[k, 1, pl.ds(x, 1), :] = p[x, PAD + width_y - 1 : PAD + width_y, :]
            return carry

        lax.fori_loop(0, width_x, stage, 0, unroll=4)

    def send_rows(k):
        for b in (1, -1):
            begin(0, b, field_y(k, b))

    loads[0].wait()
    loads[1].wait()
    stage_planes(0)
    stage_rows(0)
    pl.semaphore_wait(barrier, len(around) + 1)

    lane = lax.broadcasted_iota(jnp.int32, (CHUNK, depth), 1)
    has_above = lane < depth - 1
    has_below = lane > 0

    def above(v):
        return jnp.where(has_above, pltpu.roll(v, depth - 1, 1), 0.0)

    def below(v):
        return jnp.where(has_below, pltpu.roll(v, 1, 1), 0.0)

    def plane(k, x, before, after):
        p, q = fields[k], qs[k]
        old_p, old_q = (fields[1], qs[1]) if k == 0 else (fields[k - 1], qs[k - 1])
        new_p, new_q = fields[k + 1], qs[k + 1]
        pad = pads[k + 1]
        for y in range(0, width_y, CHUNK):
            own_rows = slice(y, y + CHUNK)
            pad_rows = slice(PAD + y, PAD + y + CHUNK)
            pc = p[x, pad_rows, :]
            lateral = (
                after(0, y)
                + before(0, y)
                + p[x, PAD + y + 1 : PAD + y + 1 + CHUNK, :]
                + p[x, PAD + y - 1 : PAD + y - 1 + CHUNK, :]
                - 4.0 * pc
            )
            qc = q[x, own_rows, :]
            slope = 0.25 * (after(1, y) - before(1, y))
            second = above(qc) + below(qc) - 2.0 * qc
            mixed = above(slope) - below(slope)
            added = inj[k, x, own_rows, :]
            upright = cv[x, own_rows, :] * (second + ct[x, own_rows, :] * mixed) + added
            horizontal = ch[x, own_rows, :] * lateral
            new_p[x, pad + y : pad + y + CHUNK, :] = (2.0 * pc - old_p[x, pad_rows, :]) + horizontal + upright
            new_q[x, own_rows, :] = (
                (2.0 * qc - old_q[x, own_rows, :])
                + cr[x, own_rows, :] * horizontal
                + upright
            )

    def near(k, x):
        p, q = fields[k], qs[k]

        def get(which, y):
            if which == 0:
                return p[x, PAD + y : PAD + y + CHUNK, :]
            return q[x, y : y + CHUNK, :]

        return get

    def far(k, side):
        def get(which, y):
            return xrecv[k, side, which, y : y + CHUNK, :].astype(jnp.float32)

        return get

    def mend(k):
        new_p, new_q, pad = fields[k + 1], qs[k + 1], pads[k + 1]

        def one(x, carry):
            for side, y in ((0, 0), (1, width_y - 1)):
                part = ch[x, y : y + 1, :] * yrecv[k, side, pl.ds(x, 1), :]
                line = new_p[x, pad + y : pad + y + 1, :] + part
                new_p[x, pad + y : pad + y + 1, :] = line
                if k < NT - 1:
                    ysend[k + 1, side, pl.ds(x, 1), :] = line
                new_q[x, y : y + 1, :] += cr[x, y : y + 1, :] * part
            return carry

        for x in (0, last):
            one(x, 0)
        if k < NT - 1:
            stage_planes(k + 1)
            send_planes(k + 1)
        lax.fori_loop(1, last, one, 0, unroll=3)
        if k < NT - 1:
            send_rows(k + 1)

    send_planes(0)
    send_rows(0)
    for j in range(2):
        to_peer(j, 0).start()
    for j in range(2):
        for a in sides:
            for b in (1, -1):
                begin(a, b, source_corner(j, a, b))
        for b in (1, -1):
            begin(0, b, source_y(j, b))
    for copy in loads[2:]:
        copy.wait()

    for k in range(NT):
        mine = pieces[k // 2]
        half = (len(mine) + 1) // 2
        for j, a, part in mine[half:] if k % 2 else mine[:half]:
            begin(a, 0, source_x(j, a, part))

        def inner(x, carry, k=k):
            plane(k, x, near(k, x - 1), near(k, x + 1))
            return carry

        lax.fori_loop(1, last, inner, 0)
        for side in (1, -1):
            landed(side, 0, field_x(k, side))
        plane(k, 0, far(k, 0), near(k, 1))
        plane(k, last, near(k, last - 1), far(k, 1))
        for side in (1, -1):
            landed(0, side, field_y(k, side))
        mend(k)

    for j, a, part in pieces[0]:
        landed(a, 0, source_x(j, a, part))
    for part in halves:
        to_peer(0, part).start()
    for j in range(2):
        for b in (1, -1):
            landed(0, b, source_y(j, b))
            for a in sides:
                landed(a, b, source_corner(j, a, b))
        for part in (3, 4):
            to_peer(j, part).start()
    for j, a, part in pieces[1]:
        landed(a, 0, source_x(j, a, part))
    for part in halves:
        to_peer(1, part).start()
    for part in parts:
        for j in range(2):
            to_peer(j, part).wait_recv()

    shift_x = lag[0, 0]
    shift_y = lag[0, 1]

    def times(s):
        return (2 * mem + s) if s < 2 else (2 * (1 - mem) + s - 2)

    def imaging(low):
        def by_plane(x, carry):
            at_x = x + HMAX - shift_x
            for s in range(4):
                wide[s, 0:HMAX, :] = yl[s][at_x].astype(jnp.float32)
                wide[s, HMAX : HMAX + width_y, :] = sx[s][at_x].astype(jnp.float32)
                wide[s, HMAX + width_y : 2 * HMAX + width_y, :] = yr[s][at_x].astype(
                    jnp.float32
                )
            for y in range(0, width_y, CHUNK):
                total = None
                for s in range(4):
                    k = NT - 1 - ((2 * low + s) if s < 2 else (2 * (1 - low) + s - 2))
                    piece = wide[s, pl.ds(HMAX - shift_y + y, CHUNK), :]
                    term = piece * fields[k][x, PAD + y : PAD + y + CHUNK, :]
                    total = term if total is None else total + term
                image_out[0, x, y : y + CHUNK, :] = total
            return carry

        lax.fori_loop(0, width_x, by_plane, 0)

    for m in range(2):

        @pl.when(mem == m)
        def _(m=m):
            imaging(m)

    for k in range(NT):
        for a in (1, -1):
            sent(a, 0, field_x(k, a))
            sent(0, a, field_y(k, a))
    for j in range(2):
        for piece in pieces[j]:
            sent(piece[1], 0, source_x(*piece))
        for b in (1, -1):
            sent(0, b, source_y(j, b))
            for a in sides:
                sent(a, b, source_corner(j, a, b))
        for part in parts:
            to_peer(j, part).wait_send()


def land_kernel(*refs):
    sem = refs[-1]
    count = len(refs) // 2
    copies = [
        pltpu.make_async_copy(refs[i], refs[count + i], sem.at[i]) for i in range(count)
    ]
    for copy in copies:
        copy.start()
    for copy in copies:
        copy.wait()


def land(*results):
    return pl.pallas_call(
        land_kernel,
        out_shape=tuple(jax.ShapeDtypeStruct(r.shape, r.dtype) for r in results),
        in_specs=[pl.BlockSpec(memory_space=pl.ANY)] * len(results),
        out_specs=tuple(pl.BlockSpec(memory_space=pltpu.HBM) for r in results),
        scratch_shapes=[pltpu.SemaphoreType.DMA((len(results),))],
        compiler_params=pltpu.CompilerParams(vmem_limit_bytes=1 << 20),
        name="land",
    )(*results)


def march(counts, reach, lag, src, rec_p, rec_q, prev_p, prev_q, horiz, vert, ratio, tilt, inj):
    shape = rec_p.shape
    width_x, width_y, depth = shape
    padded = (width_x, width_y + 2 * PAD, depth)
    f32, bf16 = jnp.float32, jnp.bfloat16
    hbm = pl.BlockSpec(memory_space=pltpu.HBM)
    vmem = pl.BlockSpec(memory_space=pltpu.VMEM)
    scratch = (
        [pltpu.VMEM(padded, f32)] * 4
        + [pltpu.VMEM(shape, f32)] * 2
        + [pltpu.VMEM(shape, f32)] * 4
        + [pltpu.VMEM((width_x + 2 * HMAX, width_y, depth), bf16)] * 4
        + [pltpu.VMEM((width_x + 2 * HMAX, HMAX, depth), bf16)] * 8
        + [pltpu.VMEM((4, width_y + 2 * HMAX, depth), f32)]
        + [pltpu.VMEM((NT, 2, 2, width_y, depth), bf16)] * 2
        + [pltpu.VMEM((NT, 2, width_x, depth), f32)] * 2
        + [pltpu.SemaphoreType.DMA((10,))]
        + [pltpu.SemaphoreType.DMA((2, n)) for n in (8, 4, 8, 10, 2 * NT, 2 * NT)]
    )
    return land(*pl.pallas_call(
        functools.partial(march_kernel, counts, reach),
        out_shape=(
            jax.ShapeDtypeStruct((1,) + shape, f32),
            jax.ShapeDtypeStruct(shape, f32),
            jax.ShapeDtypeStruct(shape, f32),
        ),
        in_specs=[pl.BlockSpec(memory_space=pltpu.SMEM)] + [hbm] * 9 + [vmem],
        out_specs=(vmem, vmem, vmem),
        scratch_shapes=scratch,
        compiler_params=pltpu.CompilerParams(
            collective_id=REACHES.index(reach), has_side_effects=True, vmem_limit_bytes=38 << 20
        ),
        name=f"march{reach}",
    )(lag, src, rec_p, rec_q, prev_p, prev_q, horiz, vert, ratio, tilt, inj))


def solution(mesh):
    counts = (mesh.shape["gx"], mesh.shape["gy"])

    def body(
        src_hist, rec_p, rec_q, prev_p, prev_q, horiz, vert, ratio, tilt, rec_pos, rec_data, lag_offs
    ):
        added = inject(counts, rec_pos, rec_data, rec_p.shape)
        other = lax.ppermute(lag_offs, "mem", [(0, 1), (1, 0)])
        need = -jnp.minimum(lag_offs[0, 0], other[0, 0])
        branch = sum((need > r).astype(jnp.int32) for r in REACHES[:-1])
        return lax.switch(
            branch,
            [functools.partial(march, counts, r) for r in REACHES],
            lag_offs, src_hist, rec_p, rec_q, prev_p, prev_q, horiz, vert, ratio, tilt, added,
        )

    cells = P("gx", "gy", None)
    return jax.shard_map(
        body,
        mesh=mesh,
        in_specs=(P("mem", "gx", "gy", None),) + (cells,) * 8 + (P(), P(), P("mem", None)),
        out_specs=(P("mem", "gx", "gy", None), cells, cells),
        check_vma=False,
    )
```

```python
import functools

import jax
import jax.numpy as jnp
from jax import lax
from jax.experimental import pallas as pl
from jax.experimental.pallas import tpu as pltpu
from jax.sharding import PartitionSpec as P

NT = 4
HMAX = 8
PAD = 8
PIECE = 4
REACHES = (0, 2, 4, 6, 8)
CHUNK = 32
MESH = pl.DeviceIdType.MESH


def log2(n):
    bits = n.bit_length() - 1
    assert 1 << bits == n
    return bits


def inject_kernel(
    counts, pos_rows, pos, data, out, pos_v, pos_s, data_s, link_v, link_s, sem
):
    _, width_x, width_y, depth = out.shape
    staged = [
        pltpu.make_async_copy(here, there, sem.at[i])
        for i, (here, there) in enumerate(((pos_rows, pos_v), (pos, pos_s), (data, data_s)))
    ]
    for copy in staged:
        copy.start()

    def clear(x, carry):
        for t in range(NT):
            out[t, x] = jnp.zeros((width_y, depth), jnp.float32)
        return carry

    lax.fori_loop(0, width_x // 2, clear, 0)
    rows = pos_v.shape[0]
    total = rows * 128
    bits_z, bits_y, bits_x = log2(depth), log2(width_y), log2(width_x)
    bits_gy = log2(counts[1])
    staged[0].wait()
    place = pos_v[...]
    block_y = (place >> (bits_z + bits_y)) & (counts[1] - 1)
    block_x = place >> (bits_z + bits_y + bits_gy + bits_x)
    inside = (block_x == lax.axis_index("gx")) & (block_y == lax.axis_index("gy"))
    lane = lax.broadcasted_iota(jnp.int32, (rows, 128), 1)
    row = lax.broadcasted_iota(jnp.int32, (rows, 128), 0)
    link = jnp.where(inside, row * 128 + lane, total)
    step = 1
    while step < 128:
        ahead = pltpu.roll(link, 128 - step, 1)
        link = jnp.minimum(link, jnp.where(lane < 128 - step, ahead, total))
        step *= 2
    later = jnp.broadcast_to(link[:, :1], (rows, 128))
    later = jnp.where(row < rows - 1, pltpu.roll(later, rows - 1, 0), total)
    step = 1
    while step < rows:
        ahead = pltpu.roll(later, rows - step, 0)
        later = jnp.minimum(later, jnp.where(row < rows - step, ahead, total))
        step *= 2
    link_v[...] = jnp.minimum(link, later)
    copy = pltpu.make_async_copy(link_v, link_s, sem.at[3])
    copy.start()
    lax.fori_loop(width_x // 2, width_x, clear, 0)
    copy.wait()
    for copy in staged[1:]:
        copy.wait()
    cell = lax.broadcasted_iota(jnp.int32, (1, depth), 1)

    def add(r):
        where = pos_s[r]
        x = (where >> (bits_z + bits_y + bits_gy)) & (width_x - 1)
        y = (where >> bits_z) & (width_y - 1)
        z = where & (depth - 1)
        hit = cell == z
        for t in range(NT):
            line = out[t, x, pl.ds(y, 1), :]
            out[t, x, pl.ds(y, 1), :] = line + jnp.where(hit, data_s[NT - 1 - t, r], 0.0)
        after = jnp.minimum(r + 1, total - 1)
        return jnp.where(r + 1 < total, link_s[after >> 7, after & 127], total)

    lax.while_loop(lambda r: r < total, add, link_s[0, 0])


def inject(counts, rec_pos, rec_data, shape):
    total = rec_pos.shape[0]
    rows = total // 128
    return pl.pallas_call(
        functools.partial(inject_kernel, counts),
        out_shape=jax.ShapeDtypeStruct((NT,) + shape, jnp.float32),
        in_specs=[pl.BlockSpec(memory_space=pltpu.HBM)] * 3,
        out_specs=pl.BlockSpec(memory_space=pltpu.VMEM),
        scratch_shapes=[
            pltpu.VMEM((rows, 128), jnp.int32),
            pltpu.SMEM((total,), jnp.int32),
            pltpu.SMEM(rec_data.shape, jnp.float32),
            pltpu.VMEM((rows, 128), jnp.int32),
            pltpu.SMEM((rows, 128), jnp.int32),
            pltpu.SemaphoreType.DMA((4,)),
        ],
        compiler_params=pltpu.CompilerParams(vmem_limit_bytes=20 << 20),
        name="inject",
    )(
        *(
            pltpu.with_memory_space_constraint(v, pltpu.HBM)
            for v in (rec_pos.reshape(rows, 128), rec_pos, rec_data)
        )
    )


def march_kernel(
    counts,
    reach,
    lag,
    src,
    rec_p,
    rec_q,
    prev_p,
    prev_q,
    horiz,
    vert,
    ratio,
    tilt,
    inj,
    image_out,
    p_out,
    q_out,
    f0, f1, f2, f3,
    qa, qb,
    ch, cv, cr, ct,
    sx0, sx1, sx2, sx3,
    yl0, yl1, yl2, yl3,
    yr0, yr1, yr2, yr3,
    wide,
    xsend, xrecv, ysend, yrecv,
    load_sem,
    sx_sem, sy_sem, sc_sem, sm_sem,
    px_sem, py_sem, pm_sem,
):
    n_gx, n_gy = counts
    gx, gy, mem = lax.axis_index("gx"), lax.axis_index("gy"), lax.axis_index("mem")
    width_x, width_y, depth = rec_p.shape
    last = width_x - 1
    sx = (sx0, sx1, sx2, sx3)
    yl = (yl0, yl1, yl2, yl3)
    yr = (yr0, yr1, yr2, yr3)
    own = pl.ds(HMAX, width_x)
    rows_in = pl.ds(PAD, width_y)

    loads = []

    def load(source, dest):
        copy = pltpu.make_async_copy(source, dest, load_sem.at[len(loads)])
        copy.start()
        loads.append(copy)

    load(rec_p, f0.at[:, rows_in])
    load(rec_q, qa)
    load(prev_p, f1.at[:, rows_in])
    load(horiz, ch)
    load(vert, cv)
    load(tilt, ct)
    load(prev_q, qb)
    load(ratio, cr)
    load(src.at[0], sx0.at[own])
    load(src.at[1], sx1.at[own])

    def at(dgx, dgy):
        return ((gx + dgx + n_gx) % n_gx, (gy + dgy + n_gy) % n_gy, mem)

    peer = (gx, gy, 1 - mem)
    barrier = pltpu.get_barrier_semaphore()
    around = [(a, b) for a in (-1, 0, 1) for b in (-1, 0, 1) if (a, b) != (0, 0)]
    for a, b in around:
        pl.semaphore_signal(barrier, inc=1, device_id=at(a, b), device_id_type=MESH)
    pl.semaphore_signal(barrier, inc=1, device_id=peer, device_id_type=MESH)

    def exists(a, b):
        ok = True
        if a == -1:
            ok = gx > 0
        if a == 1:
            ok = gx < n_gx - 1
        if b == -1:
            ok_y = gy > 0
        if b == 1:
            ok_y = gy < n_gy - 1
        if b == 0:
            return ok
        if a == 0:
            return ok_y
        return ok & ok_y

    zero_row = jnp.zeros((1, depth), jnp.float32)

    def clear_pads(x, carry):
        for f in (f0, f1, f2, f3):
            f[x, PAD - 1 : PAD, :] = zero_row
            f[x, PAD + width_y : PAD + width_y + 1, :] = zero_row
        return carry

    lax.fori_loop(0, width_x, clear_pads, 0)

    spans = {-1: (0, HMAX), 0: (HMAX, width_x), 1: (HMAX + width_x, reach)}
    sides = (1, -1) if reach else (1,)
    for j in range(2):
        for a in (-1, 1):
            first, n = spans[a]

            @pl.when(jnp.logical_not(exists(a, 0)))
            def _(j=j, first=first, n=n):
                for x in range(n):
                    sx[j][first + x] = jnp.zeros((width_y, depth), jnp.bfloat16)

        for b, side in ((-1, yl), (1, yr)):
            for a in (-1, 0, 1):
                first, n = spans[a]
                if not n:
                    continue

                @pl.when(jnp.logical_not(exists(a, b)))
                def _(j=j, first=first, n=n, side=side):
                    def clear(x, carry):
                        side[j][first + x] = jnp.zeros((HMAX, depth), jnp.bfloat16)
                        return carry

                    lax.fori_loop(0, n, clear, 0)

    for a, side in ((-1, 0), (1, 1)):

        @pl.when(jnp.logical_not(exists(a, 0)))
        def _(side=side):
            for k in range(NT):
                for f in range(2):
                    xrecv[k, side, f] = jnp.zeros((width_y, depth), jnp.bfloat16)

        @pl.when(jnp.logical_not(exists(0, a)))
        def _(side=side):
            for k in range(NT):
                yrecv[k, side] = jnp.zeros((width_x, depth), jnp.float32)

    def remote(source, dest, sems, i, target):
        return pltpu.make_async_remote_copy(
            src_ref=source,
            dst_ref=dest,
            send_sem=sems.at[0, i],
            recv_sem=sems.at[1, i],
            device_id=target,
            device_id_type=MESH,
        )

    def begin(a, b, copy):
        @pl.when(exists(a, b))
        def _():
            copy().start()

    def sent(a, b, copy):
        @pl.when(exists(a, b))
        def _():
            copy().wait_send()

    def landed(a, b, copy):
        @pl.when(exists(-a, -b))
        def _():
            copy().wait_recv()

    def edge_x(a):
        return pl.ds(width_x - HMAX, HMAX) if a == 1 else pl.ds(0, reach)

    def edge_y(b):
        return pl.ds(width_y - HMAX, HMAX) if b == 1 else pl.ds(0, HMAX)

    def halo_x(a):
        first, n = spans[-a]
        return pl.ds(first, n)

    def source_x(j, a, part):
        i = j * 4 + (a + 1) + part
        first = width_x - HMAX if a == 1 else 0
        size = min(PIECE, spans[-a][1] - part * PIECE)
        return lambda: remote(
            src.at[j, pl.ds(first + part * PIECE, size)],
            sx[j].at[pl.ds(spans[-a][0] + part * PIECE, size)],
            sx_sem,
            i,
            at(a, 0),
        )

    halves = (1, 2) if reach else (1,)
    parts = (0,) + halves + (3, 4)
    pieces = [
        [(j, a, part) for part in range(2) for a in sides if part * PIECE < spans[-a][1]]
        for j in range(2)
    ]

    def source_y(j, b):
        i = j * 2 + (b + 1) // 2
        dest = yl if b == 1 else yr
        return lambda: remote(
            src.at[j, :, edge_y(b)], dest[j].at[own], sy_sem, i, at(0, b)
        )

    def source_corner(j, a, b):
        i = j * 4 + (a + 1) + (b + 1) // 2
        dest = yl if b == 1 else yr
        return lambda: remote(
            src.at[j, edge_x(a), edge_y(b)],
            dest[j].at[halo_x(a)],
            sc_sem,
            i,
            at(a, b),
        )

    def to_peer(j, part):
        if part == 0:
            return remote(src.at[j], sx[2 + j].at[own], sm_sem, j, peer)
        if part == 1:
            here, there = sx[j].at[pl.ds(*spans[-1])], sx[2 + j].at[pl.ds(*spans[-1])]
        if part == 2:
            here, there = sx[j].at[pl.ds(*spans[1])], sx[2 + j].at[pl.ds(*spans[1])]
        used = pl.ds(0, HMAX + width_x + reach)
        if part == 3:
            here, there = yl[j].at[used], yl[2 + j].at[used]
        if part == 4:
            here, there = yr[j].at[used], yr[2 + j].at[used]
        return remote(here, there, sm_sem, part * 2 + j, peer)

    def field_x(k, a):
        side = (a + 1) // 2
        return lambda: remote(
            xsend.at[k, side], xrecv.at[k, 1 - side, mem], px_sem, k * 2 + side, at(a, 0)
        )

    def shared_x(k, a):
        side = (a + 1) // 2
        here = xrecv.at[k, 1 - side, mem]
        return lambda: remote(here, here, pm_sem, k * 2 + side, peer)

    def field_y(k, b):
        side = (b + 1) // 2
        return lambda: remote(
            ysend.at[k, side], yrecv.at[k, 1 - side], py_sem, k * 2 + side, at(0, b)
        )

    fields = (f0, f1, f2, f3, p_out)
    qs = (qa, qb, qa, qb, q_out)
    pads = (PAD, PAD, PAD, PAD, 0)

    def stage_planes(k):
        p, q = fields[k], qs[k]
        for side, x in ((0, 0), (1, last)):

            @pl.when(mem == 0)
            def _(side=side, x=x):
                xsend[k, side] = p[x, PAD : PAD + width_y, :].astype(jnp.bfloat16)

            @pl.when(mem == 1)
            def _(side=side, x=x):
                xsend[k, side] = q[x].astype(jnp.bfloat16)

    def send_planes(k):
        for a in (1, -1):
            begin(a, 0, field_x(k, a))

    def stage_rows(k):
        p = fields[k]

        def stage(x, carry):
            ysend[k, 0, pl.ds(x, 1), :] = p[x, PAD : PAD + 1, :]
            ysend[k, 1, pl.ds(x, 1), :] = p[x, PAD + width_y - 1 : PAD + width_y, :]
            return carry

        lax.fori_loop(0, width_x, stage, 0, unroll=4)

    def send_rows(k):
        for b in (1, -1):
            begin(0, b, field_y(k, b))

    loads[0].wait()
    loads[1].wait()
    stage_planes(0)
    stage_rows(0)
    pl.semaphore_wait(barrier, len(around) + 1)

    lane = lax.broadcasted_iota(jnp.int32, (CHUNK, depth), 1)
    has_above = lane < depth - 1
    has_below = lane > 0

    def above(v):
        return jnp.where(has_above, pltpu.roll(v, depth - 1, 1), 0.0)

    def below(v):
        return jnp.where(has_below, pltpu.roll(v, 1, 1), 0.0)

    def plane(k, x, before, after):
        p, q = fields[k], qs[k]
        old_p, old_q = (fields[1], qs[1]) if k == 0 else (fields[k - 1], qs[k - 1])
        new_p, new_q = fields[k + 1], qs[k + 1]
        pad = pads[k + 1]
        for y in range(0, width_y, CHUNK):
            own_rows = slice(y, y + CHUNK)
            pad_rows = slice(PAD + y, PAD + y + CHUNK)
            pc = p[x, pad_rows, :]
            lateral = (
                after(0, y)
                + before(0, y)
                + p[x, PAD + y + 1 : PAD + y + 1 + CHUNK, :]
                + p[x, PAD + y - 1 : PAD + y - 1 + CHUNK, :]
                - 4.0 * pc
            )
            qc = q[x, own_rows, :]
            slope = 0.25 * (after(1, y) - before(1, y))
            second = above(qc) + below(qc) - 2.0 * qc
            mixed = above(slope) - below(slope)
            added = inj[k, x, own_rows, :]
            upright = cv[x, own_rows, :] * (second + ct[x, own_rows, :] * mixed) + added
            horizontal = ch[x, own_rows, :] * lateral
            new_p[x, pad + y : pad + y + CHUNK, :] = (2.0 * pc - old_p[x, pad_rows, :]) + horizontal + upright
            new_q[x, own_rows, :] = (
                (2.0 * qc - old_q[x, own_rows, :])
                + cr[x, own_rows, :] * horizontal
                + upright
            )

    def near(k, x):
        p, q = fields[k], qs[k]

        def get(which, y):
            if which == 0:
                return p[x, PAD + y : PAD + y + CHUNK, :]
            return q[x, y : y + CHUNK, :]

        return get

    def far(k, side):
        def get(which, y):
            return xrecv[k, side, which, y : y + CHUNK, :].astype(jnp.float32)

        return get

    def mend(k):
        new_p, new_q, pad = fields[k + 1], qs[k + 1], pads[k + 1]

        def one(x, carry):
            for side, y in ((0, 0), (1, width_y - 1)):
                part = ch[x, y : y + 1, :] * yrecv[k, side, pl.ds(x, 1), :]
                line = new_p[x, pad + y : pad + y + 1, :] + part
                new_p[x, pad + y : pad + y + 1, :] = line
                if k < NT - 1:
                    ysend[k + 1, side, pl.ds(x, 1), :] = line
                new_q[x, y : y + 1, :] += cr[x, y : y + 1, :] * part
            return carry

        for x in (0, last):
            one(x, 0)
        if k < NT - 1:
            stage_planes(k + 1)
            send_planes(k + 1)
        lax.fori_loop(1, last, one, 0, unroll=3)
        if k < NT - 1:
            send_rows(k + 1)

    send_planes(0)
    send_rows(0)
    for j in range(2):
        to_peer(j, 0).start()
    for j in range(2):
        for a in sides:
            for b in (1, -1):
                begin(a, b, source_corner(j, a, b))
        for b in (1, -1):
            begin(0, b, source_y(j, b))
    for copy in loads[2:]:
        copy.wait()

    def imaging(low, slots, fresh):
        def by_plane(x, carry):
            at_x = x + HMAX - lag[0, 0]
            for s in slots:
                wide[s, 0:HMAX, :] = yl[s][at_x].astype(jnp.float32)
                wide[s, HMAX : HMAX + width_y, :] = sx[s][at_x].astype(jnp.float32)
                wide[s, HMAX + width_y : 2 * HMAX + width_y, :] = yr[s][at_x].astype(
                    jnp.float32
                )
            for y in range(0, width_y, CHUNK):
                total = None if fresh else image_out[0, x, y : y + CHUNK, :]
                for s in slots:
                    k = NT - 1 - ((2 * low + s) if s < 2 else (2 * (1 - low) + s - 2))
                    piece = wide[s, pl.ds(HMAX - lag[0, 1] + y, CHUNK), :]
                    term = piece * fields[k][x, PAD + y : PAD + y + CHUNK, :]
                    total = term if total is None else total + term
                image_out[0, x, y : y + CHUNK, :] = total
            return carry

        lax.fori_loop(0, width_x, by_plane, 0)

    def image_slots(slots, fresh):
        for m in range(2):

            @pl.when(mem == m)
            def _(m=m):
                imaging(m, slots, fresh)

    def forward(j):
        for piece in pieces[j]:
            landed(piece[1], 0, source_x(*piece))
        for part in halves:
            to_peer(j, part).start()
        for b in (1, -1):
            landed(0, b, source_y(j, b))
            for a in sides:
                landed(a, b, source_corner(j, a, b))
        for part in (3, 4):
            to_peer(j, part).start()

    def collect(j):
        for part in parts:
            to_peer(j, part).wait_recv()

    early = reach == 0
    for k in range(NT):
        mine = pieces[k // 2]
        half = (len(mine) + 1) // 2
        for j, a, part in mine[half:] if k % 2 else mine[:half]:
            begin(a, 0, source_x(j, a, part))

        def inner(x, carry, k=k):
            plane(k, x, near(k, x - 1), near(k, x + 1))
            return carry

        lax.fori_loop(1, last, inner, 0)
        if early and k == NT - 1:
            collect(0)
            image_slots((0, 2), True)
        for side in (1, -1):
            landed(side, 0, field_x(k, side))
            begin(-side, 0, shared_x(k, side))
        for side in (1, -1):
            landed(side, 0, shared_x(k, side))
        plane(k, 0, far(k, 0), near(k, 1))
        plane(k, last, near(k, last - 1), far(k, 1))
        for side in (1, -1):
            landed(0, side, field_y(k, side))
        mend(k)
        if early and k == NT - 2:
            forward(0)

    if early:
        forward(1)
        collect(1)
        image_slots((1, 3), False)
    else:
        forward(0)
        forward(1)
        collect(0)
        collect(1)
        image_slots((0, 1, 2, 3), True)

    for k in range(NT):
        for a in (1, -1):
            sent(a, 0, field_x(k, a))
            sent(-a, 0, shared_x(k, a))
            sent(0, a, field_y(k, a))
    for j in range(2):
        for piece in pieces[j]:
            sent(piece[1], 0, source_x(*piece))
        for b in (1, -1):
            sent(0, b, source_y(j, b))
            for a in sides:
                sent(a, b, source_corner(j, a, b))
        for part in parts:
            to_peer(j, part).wait_send()


def land_kernel(*refs):
    sem = refs[-1]
    count = len(refs) // 2
    copies = [
        pltpu.make_async_copy(refs[i], refs[count + i], sem.at[i]) for i in range(count)
    ]
    for copy in copies:
        copy.start()
    for copy in copies:
        copy.wait()


def land(*results):
    return pl.pallas_call(
        land_kernel,
        out_shape=tuple(jax.ShapeDtypeStruct(r.shape, r.dtype) for r in results),
        in_specs=[pl.BlockSpec(memory_space=pl.ANY)] * len(results),
        out_specs=tuple(pl.BlockSpec(memory_space=pltpu.HBM) for r in results),
        scratch_shapes=[pltpu.SemaphoreType.DMA((len(results),))],
        compiler_params=pltpu.CompilerParams(vmem_limit_bytes=1 << 20),
        name="land",
    )(*results)


def march(counts, reach, lag, src, rec_p, rec_q, prev_p, prev_q, horiz, vert, ratio, tilt, inj):
    shape = rec_p.shape
    width_x, width_y, depth = shape
    padded = (width_x, width_y + 2 * PAD, depth)
    f32, bf16 = jnp.float32, jnp.bfloat16
    hbm = pl.BlockSpec(memory_space=pltpu.HBM)
    vmem = pl.BlockSpec(memory_space=pltpu.VMEM)
    scratch = (
        [pltpu.VMEM(padded, f32)] * 4
        + [pltpu.VMEM(shape, f32)] * 2
        + [pltpu.VMEM(shape, f32)] * 4
        + [pltpu.VMEM((width_x + 2 * HMAX, width_y, depth), bf16)] * 4
        + [pltpu.VMEM((width_x + 2 * HMAX, HMAX, depth), bf16)] * 8
        + [pltpu.VMEM((4, width_y + 2 * HMAX, depth), f32)]
        + [pltpu.VMEM((NT, 2, width_y, depth), bf16), pltpu.VMEM((NT, 2, 2, width_y, depth), bf16)]
        + [pltpu.VMEM((NT, 2, width_x, depth), f32)] * 2
        + [pltpu.SemaphoreType.DMA((10,))]
        + [pltpu.SemaphoreType.DMA((2, n)) for n in (8, 4, 8, 10, 2 * NT, 2 * NT, 2 * NT)]
    )
    return land(*pl.pallas_call(
        functools.partial(march_kernel, counts, reach),
        out_shape=(
            jax.ShapeDtypeStruct((1,) + shape, f32),
            jax.ShapeDtypeStruct(shape, f32),
            jax.ShapeDtypeStruct(shape, f32),
        ),
        in_specs=[pl.BlockSpec(memory_space=pltpu.SMEM)] + [hbm] * 9 + [vmem],
        out_specs=(vmem, vmem, vmem),
        scratch_shapes=scratch,
        compiler_params=pltpu.CompilerParams(
            collective_id=REACHES.index(reach), has_side_effects=True, vmem_limit_bytes=38 << 20
        ),
        name=f"march{reach}",
    )(lag, src, rec_p, rec_q, prev_p, prev_q, horiz, vert, ratio, tilt, inj))


def solution(mesh):
    counts = (mesh.shape["gx"], mesh.shape["gy"])

    def body(
        src_hist, rec_p, rec_q, prev_p, prev_q, horiz, vert, ratio, tilt, rec_pos, rec_data, lag_offs
    ):
        added = inject(counts, rec_pos, rec_data, rec_p.shape)
        other = lax.ppermute(lag_offs, "mem", [(0, 1), (1, 0)])
        need = -jnp.minimum(lag_offs[0, 0], other[0, 0])
        branch = sum((need > r).astype(jnp.int32) for r in REACHES[:-1])
        return lax.switch(
            branch,
            [functools.partial(march, counts, r) for r in REACHES],
            lag_offs, src_hist, rec_p, rec_q, prev_p, prev_q, horiz, vert, ratio, tilt, added,
        )

    cells = P("gx", "gy", None)
    return jax.shard_map(
        body,
        mesh=mesh,
        in_specs=(P("mem", "gx", "gy", None),) + (cells,) * 8 + (P(), P(), P("mem", None)),
        out_specs=(P("mem", "gx", "gy", None), cells, cells),
        check_vma=False,
    )
```
